256 devices in a mesh: dp: 4 (over y), pipe: 4 (over z_hi), tensor: 16 (over x, z_lo, core).
Axes of the slice: x: 4, y: 4, z: 8 (z_hi: 4, z_lo: 2; z = z_hi * 2 + z_lo), core: 2. Of those that a mesh axis runs over, the one named last changes fastest.
Arguments:
- hidden: bfloat16 [4, 2048, 14336], P('pipe', 'dp', 'tensor'), parts along dimension 1, may hold values from -6 to 6
- residual: bfloat16 [4, 2048, 4096], P('pipe', ('dp', 'tensor')), parts along dimension 1, may hold values from -6 to 6
- norm_gain: float32 [4, 4096], P('pipe'), may hold values from 0.5 to 1.5
- down_weight: bfloat16 [4, 14336, 4096], P('pipe', 'tensor'), may hold values from -0.046875 to 0.046875
- qkv_weight: bfloat16 [4, 4096, 6144], P('pipe', None, 'tensor'), may hold values from -0.09375 to 0.09375
Outputs:
- section_output: bfloat16 [4, 2048, 4096], P('pipe', ('dp', 'tensor')), parts along dimension 1
- projections: bfloat16 [4, 2048, 6144], P('pipe', 'dp', 'tensor'), parts along dimension 1
The draws below stay inside these ranges and needn't reach their ends.
There are 4 independent parts, one for each index of `dp`. The reference program is written for one: setup_inputs(seed, part) draws one part's arguments, and reference() takes and returns one part's arrays. A program takes and returns all parts, laid end to end along the dimension named above; an argument that names none is the same for every part. Nothing has to cross between parts.
All inputs are finite; a program needn't handle non-finite values.
Results may differ from the reference program's by a relative error of at most 0.022.
Values may be sent and summed in bfloat16 or wider, within the bound.
No kernel may reach another device: no remote copies, remote signals or barrier semaphores. Data moves between devices by JAX's collectives and lax.ppermute only.
A program may use at most 64 MiB of HBM per device.

```python
import jax
import jax.numpy as jnp
from jax import lax

D = 4096
FF = 14336
TOKENS = 512
QKV = 6144
SECTIONS = 4
N_TENSOR = 16


def block_levels(stream_key, extent, pieces, smallest, high):
    level = 1.0
    for position, shards_of in pieces:
        heights = jax.random.uniform(jax.random.fold_in(jax.random.fold_in(stream_key, 6), position), (shards_of,), jnp.float32, smallest / len(pieces), high / len(pieces))
        level = level * jnp.repeat(jnp.exp(heights), extent[position] // shards_of).reshape((-1,) + (1,) * (len(extent) - 1 - position))
    return level


def normal_values(rng, shape, width, limit, shards=(), kind=jnp.bfloat16):
    factor_of = block_levels(rng, shape, shards, -0.22, 0.18) if shards else 1.0
    entries = jax.random.normal(rng, shape, jnp.float32) * width * factor_of
    return jnp.minimum(jnp.maximum(entries, -limit), limit).astype(kind)


def setup_inputs(seed: int = 0, part: int = 0) -> dict:
    key_of = jax.random.split(jax.random.key(seed), 6)
    part_splits = jax.random.split(jax.random.fold_in(key_of[5], part), 6)
    return {
        "hidden": normal_values(part_splits[0], (SECTIONS, TOKENS, FF), 1.0, 6.0, ((0, 4), (2, 16))),
        "residual": normal_values(part_splits[1], (SECTIONS, TOKENS, D), 1.0, 6.0, ((0, 4), (1, 16))),
        "norm_gain": jnp.clip(1.0 + 0.1 * jax.random.normal(key_of[2], (SECTIONS, D), jnp.float32), 0.5, 1.5),
        "down_weight": normal_values(key_of[3], (SECTIONS, FF, D), FF ** -0.5, 0.046875, ((0, 4), (1, 16))),
        "qkv_weight": normal_values(key_of[4], (SECTIONS, D, QKV), D ** -0.5, 0.09375, ((0, 4), (2, 16))),
    }


def normalize(values, gain_row):
    wide = values.astype(jnp.float32)
    scaler = lax.rsqrt(lax.optimization_barrier(jnp.mean(wide * wide, axis=-1, keepdims=True)) + 1e-05)
    return (wide * scaler * gain_row.astype(jnp.float32)).astype(jnp.bfloat16)

def reference(hidden, residual, norm_gain, down_weight, qkv_weight):
    group_width = FF // N_TENSOR
    outputs = []
    for section_idx in range(SECTIONS):
        hidden_rows = hidden[section_idx]
        down_local = down_weight[section_idx]

        def add_group(running, group_idx):
            offset = (group_idx * group_width).astype(jnp.int32)
            group_term = jnp.dot(lax.dynamic_slice_in_dim(hidden_rows, offset, group_width, 1), lax.dynamic_slice_in_dim(down_local, offset, group_width, 0), preferred_element_type=jnp.float32)
            group_term = lax.optimization_barrier(group_term.astype(jnp.bfloat16)).astype(jnp.float32)
            return (running + group_term, None)
        running, _ = lax.scan(add_group, jnp.zeros((TOKENS, D), jnp.float32), jnp.arange(N_TENSOR, dtype=jnp.int32))
        outputs.append((residual[section_idx].astype(jnp.float32) + running).astype(jnp.bfloat16))
    section_output = jnp.stack(outputs)
    projected = []
    for section_idx in range(SECTIONS):
        normed = normalize(section_output[(section_idx - 1) % SECTIONS], norm_gain[section_idx])
        projected.append(jnp.dot(normed, qkv_weight[section_idx], preferred_element_type=jnp.float32).astype(jnp.bfloat16))
    return (section_output, jnp.stack(projected))
```

```python
import functools
import itertools

import jax
import jax.numpy as jnp
from jax import lax
from jax.experimental import pallas as pl
from jax.experimental.pallas import tpu as pltpu
from jax.sharding import Mesh, PartitionSpec as P

CHUNKS = 2
AXES = ("x", "zl", "core")
SIZES = (4, 2, 2)


def move(value, x_mask=(0, 0), z_mask=0, core_mask=0):
    pairs = []
    for x, z, c in itertools.product(*map(range, SIZES)):
        to = ((x ^ x_mask[c]) * 2 + (z ^ z_mask)) * 2 + (c ^ core_mask)
        pairs.append(((x * 2 + z) * 2 + c, to))
    return lax.ppermute(value, AXES, pairs)


first_x = functools.partial(move, x_mask=(1, 3))
second_x = functools.partial(move, x_mask=(3, 1))
swap_z = functools.partial(move, z_mask=1)
swap_core = functools.partial(move, core_mask=1)


TRADES = {"x1": first_x, "x2": second_x, "z": swap_z}


def next_section(value):
    count = lax.axis_size("pipe")
    return lax.ppermute(value, "pipe", [(s, (s + 1) % count) for s in range(count)])


def normalize(values, gain_row):
    wide = values.astype(jnp.float32)
    scaler = lax.rsqrt(jnp.mean(wide * wide, axis=-1, keepdims=True) + 1e-05)
    return (wide * scaler * gain_row).astype(jnp.bfloat16)


def block_ids(orders):
    x, z, core = (lax.axis_index(a) for a in AXES)
    here = (x * 2 + z) * 2 + core
    near, far = 1 + 2 * core, 3 - 2 * core
    masks = ({"x1": near * 4, "x2": far * 4, "z": 2}, {"x1": far * 4, "x2": near * 4, "z": 2})
    ids = []
    for order in orders:
        for other in (0, 1):
            for p in range(8):
                t = here ^ other
                for bit, name in enumerate(reversed(order)):
                    if p >> bit & 1:
                        t = t ^ masks[other][name]
                ids.append(t)
    return jnp.stack(ids).astype(jnp.int32)


def order_kernel(ids, hid_ref, w_ref, theirs_ref, mine_ref, w_out, hid_sem, w_sem):
    rows = hid_ref.shape[0] // (16 * CHUNKS)
    parts = w_sem.shape[0]
    deep = w_ref.shape[0] // parts
    copies = []
    for i in range(parts):
        at = pl.ds(i * deep, deep)
        copies.append(pltpu.make_async_copy(w_ref.at[at, :], w_out.at[at, :], w_sem.at[i]))
    for i in range(16 * CHUNKS):
        k, other, p = i // 16, i // 8 % 2, i % 8
        start = pl.multiple_of((ids[i] * CHUNKS + k) * rows, rows)
        out = theirs_ref if other else mine_ref
        copies.append(
            pltpu.make_async_copy(
                hid_ref.at[pl.ds(start, rows), :],
                out.at[pl.ds((k * 8 + p) * rows, rows), :],
                hid_sem.at[i],
            )
        )
    for c in copies:
        c.start()
    for c in copies:
        c.wait()


def in_exchange_order(ids, hid, w, parts=8):
    rows, depth = hid.shape
    return pl.pallas_call(
        order_kernel,
        out_shape=[jax.ShapeDtypeStruct((rows // 2, depth), jnp.bfloat16)] * 2
        + [jax.ShapeDtypeStruct(w.shape, w.dtype)],
        grid_spec=pltpu.PrefetchScalarGridSpec(
            num_scalar_prefetch=1,
            grid=(1,),
            in_specs=[pl.BlockSpec(memory_space=pltpu.HBM)] * 2,
            out_specs=[pl.BlockSpec(memory_space=pltpu.VMEM)] * 3,
            scratch_shapes=[
                pltpu.SemaphoreType.DMA((16 * CHUNKS,)),
                pltpu.SemaphoreType.DMA((parts,)),
            ],
        ),
        compiler_params=pltpu.CompilerParams(vmem_limit_bytes=12 << 20),
        cost_estimate=pl.CostEstimate(
            flops=0, bytes_accessed=4 * (rows * depth + w.size), transcendentals=0
        ),
    )(ids, hid, w)


def qkv_kernel(slots, ids, *refs):
    n = len(slots)
    parts, w_ref, (out_ref, acc) = refs[:n], refs[n], refs[-2:]
    step = pl.program_id(0)

    @pl.when(step == 0)
    def _():
        acc[...] = jnp.zeros_like(acc)

    lhs = jnp.concatenate([p[...] for p in parts], axis=0)
    acc[...] += jnp.dot(lhs, w_ref[...], preferred_element_type=jnp.float32)

    @pl.when(step == pl.num_programs(0) - 1)
    def _():
        rows = acc.shape[0] // (4 * n)
        if len(refs) > n + 3:
            out_ref[...] = refs[n + 1][...]
        for i, (k, slot) in enumerate(slots):
            for j in range(4):
                start = pl.multiple_of((ids[16 * k + slot + j] * CHUNKS + k) * rows, rows)
                out_ref[pl.ds(start, rows), :] = acc[pl.ds((i * 4 + j) * rows, rows), :].astype(jnp.bfloat16)


def qkv_rows(slots, ids, pieces, w, before=None, tile=1024):
    part, depth = pieces[0].shape
    width = w.shape[1]
    n = len(slots)
    total = CHUNKS * 4 * part
    whole = pl.BlockSpec((total, width), lambda i, ids: (0, 0))
    return pl.pallas_call(
        functools.partial(qkv_kernel, slots),
        out_shape=jax.ShapeDtypeStruct((total, width), jnp.bfloat16),
        grid_spec=pltpu.PrefetchScalarGridSpec(
            num_scalar_prefetch=1,
            grid=(depth // tile,),
            in_specs=[pl.BlockSpec((part, tile), lambda i, ids: (0, i))] * n
            + [pl.BlockSpec((tile, width), lambda i, ids: (i, 0))]
            + [whole] * (before is not None),
            out_specs=whole,
            scratch_shapes=[pltpu.VMEM((n * part, width), jnp.float32)],
        ),
        compiler_params=pltpu.CompilerParams(vmem_limit_bytes=16 << 20),
        cost_estimate=pl.CostEstimate(
            flops=2 * n * part * depth * width,
            bytes_accessed=2 * (n * part * depth + depth * width + total * width),
            transcendentals=0,
        ),
    )(ids, *pieces, w, *([] if before is None else [before]))


def dot_bf16(a, b):
    return jnp.dot(a, b, preferred_element_type=jnp.float32).astype(jnp.bfloat16)


def add(a, b):
    return (a.astype(jnp.float32) + b.astype(jnp.float32)).astype(jnp.bfloat16)


def shards(hidden, residual, norm_gain, down_weight, qkv_weight):
    resid = residual[0]
    gain = norm_gain[0]
    qkv = qkv_weight[0]
    rows = resid.shape[0] // CHUNKS
    halving = (("x1", "x2", "z"), ("z", "x1", "x2"))
    doubling = (("z", "x2", "x1"), ("z", "x2", "x1"))
    theirs, mine, down = in_exchange_order(block_ids(halving), hidden[0], down_weight[0])
    ids = block_ids([order[::-1] for order in doubling])
    rows8 = 8 * rows
    sent = lax.optimization_barrier(dot_bf16(theirs, down))
    pieces = [lax.optimization_barrier(sent[k * rows8 : (k + 1) * rows8]) for k in range(CHUNKS)]
    kept = lax.optimization_barrier(dot_bf16(mine, down))
    cur = [(kept[k * rows8 : (k + 1) * rows8], swap_core(pieces[k])) for k in range(CHUNKS)]
    for i in range(3):
        after = []
        for k, (own, got) in enumerate(cur):
            half = own.shape[0] // 2
            send = add(own[half:], got[half:])
            keep = add(own[:half], got[:half])
            after.append((keep, TRADES[halving[k][i]](send)))
        cur = after
    outs = []
    for k, (own, got) in enumerate(cur):
        base = resid[k * rows : (k + 1) * rows].astype(jnp.float32)
        if k > 0:
            own, got, _ = lax.optimization_barrier((own, got, outs[-1]))
        out = (base + (own.astype(jnp.float32) + got.astype(jnp.float32))).astype(jnp.bfloat16)
        outs.append(lax.optimization_barrier(out))
    gathered = []
    for k, o in enumerate(outs):
        came = next_section(o)
        if k > 0:
            came, _ = lax.optimization_barrier((came, gathered[-1]))
        gathered.append(normalize(came, gain))
    for i in range(2):
        gathered = [
            jnp.concatenate([g, TRADES[doubling[k][i]](g)], axis=0) for k, g in enumerate(gathered)
        ]
    a, b = gathered
    a_far, b_far = (TRADES[doubling[k][2]](g) for k, g in enumerate(gathered))
    proj = qkv_rows(
        ((0, 0), (0, 4), (0, 8), (0, 12)), ids, (a, a_far, swap_core(a), swap_core(a_far)), qkv
    )
    proj = qkv_rows(((1, 0), (1, 8)), ids, (b, swap_core(b)), qkv, proj)
    b_far, proj = lax.optimization_barrier((b_far, proj))
    proj = qkv_rows(((1, 4), (1, 12)), ids, (b_far, swap_core(b_far)), qkv, proj)
    return (jnp.concatenate(outs, axis=0)[None], proj[None])


def solution(mesh):
    fine = Mesh(mesh.devices.reshape((4, 4) + SIZES), ("dp", "pipe") + AXES)
    return jax.shard_map(
        shards,
        mesh=fine,
        in_specs=(
            P("pipe", "dp", AXES),
            P("pipe", ("dp",) + AXES, None),
            P("pipe", None),
            P("pipe", AXES, None),
            P("pipe", None, AXES),
        ),
        out_specs=(P("pipe", ("dp",) + AXES, None), P("pipe", "dp", AXES)),
        check_vma=False,
    )
```

```python
import functools
import itertools

import jax
import jax.numpy as jnp
from jax import lax
from jax.experimental import pallas as pl
from jax.experimental.pallas import tpu as pltpu
from jax.sharding import Mesh, PartitionSpec as P

AXES = ("x", "z", "core")
SIZES = (4, 2, 2)
TRADES = {
    "o": ((0, 0), 0, 0),
    "a": ((1, 3), 0, 0),
    "b": ((3, 1), 0, 0),
    "z": ((0, 0), 1, 0),
    "ab": ((2, 2), 0, 0),
    "az": ((1, 3), 1, 0),
    "bz": ((3, 1), 1, 0),
    "abz": ((2, 2), 1, 0),
    "core": ((0, 0), 0, 1),
}
FIRST = ("abz", "bz", "az", "a")
SECOND = ("ab", "b", "z", "o")
GATHERED = ("o", "ab", "a", "b", "z", "az", "abz", "bz")


def trade(value, name):
    x_mask, z_mask, core_mask = TRADES[name]
    pairs = []
    for x, z, c in itertools.product(*map(range, SIZES)):
        to = ((x ^ x_mask[c]) * 2 + (z ^ z_mask)) * 2 + (c ^ core_mask)
        pairs.append(((x * 2 + z) * 2 + c, to))
    return lax.ppermute(value, AXES, pairs)


def next_section(value):
    count = lax.axis_size("pipe")
    return lax.ppermute(value, "pipe", [(s, (s + 1) % count) for s in range(count)])


def after(value, *others):
    return lax.optimization_barrier((value,) + others)[0]


def normalize(values, gain_row):
    wide = values.astype(jnp.float32)
    scaler = lax.rsqrt(jnp.mean(wide * wide, axis=-1, keepdims=True) + 1e-05)
    return (wide * scaler * gain_row).astype(jnp.bfloat16)


def block_ids(names):
    x, z, core = (lax.axis_index(a) for a in AXES)
    ids = []
    for c in (core, 1 - core):
        for name in names:
            (m0, m1), zm, _ = TRADES[name]
            m = m0 + (m1 - m0) * c
            ids.append(((x ^ m) * 2 + (z ^ zm)) * 2 + c)
    return jnp.stack(ids).astype(jnp.int32)


def pick_kernel(ids, hid_ref, mine_ref, theirs_ref):
    rows = hid_ref.shape[0] // 16
    for i in range(16):
        start = pl.multiple_of(ids[i] * rows, rows)
        out = (mine_ref, theirs_ref)[i // 8]
        out[i % 8 * rows : (i % 8 + 1) * rows, :] = hid_ref[pl.ds(start, rows), :]


def pick(ids, hid):
    rows, depth = hid.shape
    return pl.pallas_call(
        pick_kernel,
        out_shape=[jax.ShapeDtypeStruct((rows // 2, depth), jnp.bfloat16)] * 2,
        in_specs=[pl.BlockSpec(memory_space=pltpu.SMEM), pl.BlockSpec(memory_space=pltpu.VMEM)],
        out_specs=[pl.BlockSpec(memory_space=pltpu.VMEM)] * 2,
        compiler_params=pltpu.CompilerParams(vmem_limit_bytes=4 << 20),
        cost_estimate=pl.CostEstimate(flops=0, bytes_accessed=4 * rows * depth, transcendentals=0),
    )(ids, hid)


def product(parts, w_ref):
    deep = w_ref.shape[0] // 4
    total = None
    for i in range(4):
        at = slice(i * deep, (i + 1) * deep)
        lhs = jnp.concatenate([p[:, at] for p in parts], axis=0)
        term = jnp.dot(lhs, w_ref[at, :], preferred_element_type=jnp.float32)
        total = term if total is None else total + term
    return total.astype(jnp.bfloat16)


def project_kernel(places, ids, w_ref, *refs):
    out_ref, ready_ref, rows_ref, sem = refs[-4:]
    parts = refs[:-4] if len(places) == len(refs) - 4 else refs[1:-4]
    rows = rows_ref.shape[0] // len(places)
    rows_ref[...] = product(parts, w_ref)
    copies = []
    for i, at in enumerate(places):
        start = pl.multiple_of(ids[at] * rows, rows)
        copies.append(
            pltpu.make_async_copy(
                rows_ref.at[pl.ds(i * rows, rows), :], out_ref.at[pl.ds(start, rows), :], sem.at[i]
            )
        )
    for c in copies:
        c.start()
    ready_ref[...] = jnp.zeros_like(ready_ref)
    for c in copies:
        c.wait()


def project(pieces, places, ids, w, before=None, weight=1):
    rows = pieces[0].shape[0]
    depth, width = w.shape
    n = len(pieces)
    extra = [] if before is None else [before]
    vmem = pl.BlockSpec(memory_space=pltpu.VMEM)
    anywhere = pl.BlockSpec(memory_space=pl.ANY)
    return pl.pallas_call(
        functools.partial(project_kernel, places),
        out_shape=[
            jax.ShapeDtypeStruct((16 * rows, width), jnp.bfloat16),
            jax.ShapeDtypeStruct((8, 128), jnp.float32),
        ],
        in_specs=[pl.BlockSpec(memory_space=pltpu.SMEM), vmem] + [anywhere] * len(extra) + [vmem] * n,
        out_specs=[anywhere, vmem],
        scratch_shapes=[
            pltpu.VMEM((n * rows, width), jnp.bfloat16),
            pltpu.SemaphoreType.DMA((n,)),
        ],
        input_output_aliases={2: 0} if extra else {},
        compiler_params=pltpu.CompilerParams(vmem_limit_bytes=16 << 20),
        cost_estimate=pl.CostEstimate(
            flops=weight * 2 * n * rows * depth * width,
            bytes_accessed=2 * (n * rows * depth + depth * width + n * rows * width),
            transcendentals=0,
        ),
    )(ids, w, *extra, *pieces)


def dot_bf16(a, b):
    return jnp.dot(a, b, preferred_element_type=jnp.float32).astype(jnp.bfloat16)


def add(*terms):
    return sum(t.astype(jnp.float32) for t in terms)


def shards(hidden, residual, norm_gain, down_weight, qkv_weight):
    resid = residual[0]
    gain = norm_gain[0]
    qkv = qkv_weight[0]
    down = down_weight[0]
    rows = resid.shape[0]
    half = 4 * rows
    mine, theirs = pick(block_ids(FIRST + SECOND), hidden[0])
    out_ids = block_ids(GATHERED)

    sent = lax.optimization_barrier(dot_bf16(theirs, down))
    first, second = (lax.optimization_barrier(s) for s in (sent[:half], sent[half:]))
    kept = lax.optimization_barrier(dot_bf16(mine, down))
    got = trade(first, "core")

    def both(lo, hi):
        at = slice(lo * rows, hi * rows)
        return lax.optimization_barrier(add(kept[at], got[at]).astype(jnp.bfloat16))

    abz, az_a, bz = both(0, 1), both(2, 4), both(1, 2)
    for_ab = trade(abz, "z")
    for_z_o = trade(az_a, "a")
    for_b = trade(bz, "z")
    got = trade(second, "core")
    own = [(kept[half + i * rows : half + (i + 1) * rows], got[i * rows : (i + 1) * rows]) for i in range(4)]
    ab = lax.optimization_barrier(add(*own[0], for_ab).astype(jnp.bfloat16))
    last_ab = trade(ab, "ab")
    z = lax.optimization_barrier(add(*own[2], after(for_z_o, ab)[:rows]).astype(jnp.bfloat16))
    last_z = trade(z, "z")
    b = lax.optimization_barrier(add(*own[1], after(for_b, z)).astype(jnp.bfloat16))
    last_b = trade(b, "b")
    out = add(resid, *own[3], for_z_o[rows:], last_ab, last_z, last_b).astype(jnp.bfloat16)
    out = lax.optimization_barrier(out)

    normed = lax.optimization_barrier(normalize(next_section(out), gain))
    ab = trade(normed, "ab")
    z = trade(normed, "z")
    b = trade(normed, "b")
    a = trade(normed, "a")
    az = trade(z, "a")
    abz = trade(z, "ab")
    bz = trade(b, "z")
    near = [after(t, ab, b, a) for t in (normed, ab, a, b, z)]
    near_swap = [trade(t, "core") for t in near]
    near_places = (0, 1, 2, 3, 4, 8, 9, 10, 11, 12)
    rows_near, ready = project(near + near_swap, near_places, out_ids, qkv, weight=20)
    late = [after(t, ready) for t in (az, bz, abz)]
    late_swap = [trade(t, "core") for t in late]
    late_places = (5, 7, 6, 13, 15, 14)
    proj, _ = project(late + late_swap, late_places, out_ids, qkv, before=rows_near)
    return (out[None], proj[None])


def solution(mesh):
    fine = Mesh(mesh.devices.reshape((4, 4) + SIZES), ("dp", "pipe") + AXES)
    return jax.shard_map(
        shards,
        mesh=fine,
        in_specs=(
            P("pipe", "dp", AXES),
            P("pipe", ("dp",) + AXES, None),
            P("pipe", None),
            P("pipe", AXES, None),
            P("pipe", None, AXES),
        ),
        out_specs=(P("pipe", ("dp",) + AXES, None), P("pipe", "dp", AXES)),
        check_vma=False,
    )
```

```python
import functools
import itertools

import jax
import jax.numpy as jnp
from jax import lax
from jax.experimental import pallas as pl
from jax.experimental.pallas import tpu as pltpu
from jax.sharding import Mesh, PartitionSpec as P

AXES = ("x", "z", "core")
SIZES = (4, 2, 2)
TRADES = {
    "o": ((0, 0), 0, 0),
    "a": ((1, 3), 0, 0),
    "b": ((3, 1), 0, 0),
    "z": ((0, 0), 1, 0),
    "ab": ((2, 2), 0, 0),
    "az": ((1, 3), 1, 0),
    "bz": ((3, 1), 1, 0),
    "abz": ((2, 2), 1, 0),
    "core": ((0, 0), 0, 1),
}
FIRST = ("abz", "bz", "az", "a")
SECOND = ("ab", "b", "z", "o")
GATHERED = ("o", "ab", "a", "b", "z", "az", "abz", "bz")


def trade(value, name):
    x_mask, z_mask, core_mask = TRADES[name]
    pairs = []
    for x, z, c in itertools.product(*map(range, SIZES)):
        to = ((x ^ x_mask[c]) * 2 + (z ^ z_mask)) * 2 + (c ^ core_mask)
        pairs.append(((x * 2 + z) * 2 + c, to))
    return lax.ppermute(value, AXES, pairs)


def next_section(value):
    count = lax.axis_size("pipe")
    return lax.ppermute(value, "pipe", [(s, (s + 1) % count) for s in range(count)])


def after(value, *others):
    return lax.optimization_barrier((value,) + others)[0]


def normalize(values, gain_row):
    wide = values.astype(jnp.float32)
    scaler = lax.rsqrt(jnp.mean(wide * wide, axis=-1, keepdims=True) + 1e-05)
    return (wide * scaler * gain_row).astype(jnp.bfloat16)


def block_ids(names):
    x, z, core = (lax.axis_index(a) for a in AXES)
    ids = []
    for c in (core, 1 - core):
        for name in names:
            (m0, m1), zm, _ = TRADES[name]
            m = m0 + (m1 - m0) * c
            ids.append(((x ^ m) * 2 + (z ^ zm)) * 2 + c)
    return jnp.stack(ids).astype(jnp.int32)


def pick_kernel(ids, hid_ref, mine_ref, theirs_ref):
    rows = hid_ref.shape[0] // 16
    for i in range(16):
        start = pl.multiple_of(ids[i] * rows, rows)
        out = (mine_ref, theirs_ref)[i // 8]
        out[i % 8 * rows : (i % 8 + 1) * rows, :] = hid_ref[pl.ds(start, rows), :]


def pick(ids, hid):
    rows, depth = hid.shape
    return pl.pallas_call(
        pick_kernel,
        out_shape=[jax.ShapeDtypeStruct((rows // 2, depth), jnp.bfloat16)] * 2,
        in_specs=[pl.BlockSpec(memory_space=pltpu.SMEM), pl.BlockSpec(memory_space=pltpu.VMEM)],
        out_specs=[pl.BlockSpec(memory_space=pltpu.VMEM)] * 2,
        compiler_params=pltpu.CompilerParams(vmem_limit_bytes=4 << 20),
        cost_estimate=pl.CostEstimate(flops=0, bytes_accessed=4 * rows * depth, transcendentals=0),
    )(ids, hid)


def product(parts, w_ref):
    deep = w_ref.shape[0] // 4
    total = None
    for i in range(4):
        at = slice(i * deep, (i + 1) * deep)
        lhs = jnp.concatenate([p[:, at] for p in parts], axis=0)
        term = jnp.dot(lhs, w_ref[at, :], preferred_element_type=jnp.float32)
        total = term if total is None else total + term
    return total.astype(jnp.bfloat16)


def project_kernel(places, first, ids, w_ref, *refs):
    rows_ref, sem = refs[-2:]
    parts = refs[:-4] if first else refs[1:-3]
    out_ref = refs[-4] if first else refs[-3]
    rows = rows_ref.shape[0] // len(places)
    rows_ref[...] = product(parts, w_ref)
    copies = []
    for i, at in enumerate(places):
        start = pl.multiple_of(ids[at] * rows, rows)
        copies.append(
            pltpu.make_async_copy(
                rows_ref.at[pl.ds(i * rows, rows), :], out_ref.at[pl.ds(start, rows), :], sem.at[i]
            )
        )
    for c in copies:
        c.start()
    if first:
        refs[-3][...] = jnp.zeros_like(refs[-3])
    for c in copies:
        c.wait()


def project(pieces, places, ids, w, before=None, weight=1):
    rows = pieces[0].shape[0]
    depth, width = w.shape
    n = len(pieces)
    extra = [] if before is None else [before]
    vmem = pl.BlockSpec(memory_space=pltpu.VMEM)
    anywhere = pl.BlockSpec(memory_space=pl.ANY)
    return pl.pallas_call(
        functools.partial(project_kernel, places, before is None),
        out_shape=[
            jax.ShapeDtypeStruct((16 * rows, width), jnp.bfloat16),
            jax.ShapeDtypeStruct((8, 128), jnp.float32),
        ][: 2 - len(extra)],
        in_specs=[pl.BlockSpec(memory_space=pltpu.SMEM), vmem] + [anywhere] * len(extra) + [vmem] * n,
        out_specs=[anywhere, vmem][: 2 - len(extra)],
        scratch_shapes=[
            pltpu.VMEM((n * rows, width), jnp.bfloat16),
            pltpu.SemaphoreType.DMA((n,)),
        ],
        input_output_aliases={2: 0} if extra else {},
        compiler_params=pltpu.CompilerParams(vmem_limit_bytes=16 << 20),
        cost_estimate=pl.CostEstimate(
            flops=weight * 2 * n * rows * depth * width,
            bytes_accessed=2 * (n * rows * depth + depth * width + n * rows * width),
            transcendentals=0,
        ),
    )(ids, w, *extra, *pieces)


def dot_bf16(a, b):
    return jnp.dot(a, b, preferred_element_type=jnp.float32).astype(jnp.bfloat16)


def add(*terms):
    return sum(t.astype(jnp.float32) for t in terms)


def shards(hidden, residual, norm_gain, down_weight, qkv_weight):
    resid = residual[0]
    gain = norm_gain[0]
    qkv = qkv_weight[0]
    down = down_weight[0]
    rows = resid.shape[0]
    half = 4 * rows
    mine, theirs = pick(block_ids(FIRST + SECOND), hidden[0])
    out_ids = block_ids(GATHERED)

    sent = lax.optimization_barrier(dot_bf16(theirs, down))
    first, second = (lax.optimization_barrier(s) for s in (sent[:half], sent[half:]))
    kept = lax.optimization_barrier(dot_bf16(mine, down))
    got = trade(first, "core")

    def both(lo, hi):
        at = slice(lo * rows, hi * rows)
        return lax.optimization_barrier(add(kept[at], got[at]).astype(jnp.bfloat16))

    abz, az_a, bz = both(0, 1), both(2, 4), both(1, 2)
    for_ab = trade(abz, "z")
    for_z_o = trade(az_a, "a")
    for_b = trade(bz, "z")
    got = trade(second, "core")
    own = [(kept[half + i * rows : half + (i + 1) * rows], got[i * rows : (i + 1) * rows]) for i in range(4)]
    ab = lax.optimization_barrier(add(*own[0], for_ab).astype(jnp.bfloat16))
    last_ab = trade(ab, "ab")
    z = lax.optimization_barrier(add(*own[2], after(for_z_o, ab)[:rows]).astype(jnp.bfloat16))
    last_z = trade(z, "z")
    b = lax.optimization_barrier(add(*own[1], after(for_b, z)).astype(jnp.bfloat16))
    last_b = trade(b, "b")
    out = add(resid, *own[3], for_z_o[rows:], last_ab, last_z, last_b).astype(jnp.bfloat16)
    out = lax.optimization_barrier(out)

    normed = lax.optimization_barrier(normalize(next_section(out), gain))
    b = trade(normed, "b")
    z = trade(normed, "z")
    a = trade(normed, "a")
    abz = trade(z, "ab")
    az = trade(z, "a")
    ab = trade(b, "a")
    bz = trade(b, "z")
    near = [after(t, a, b, z) for t in (normed, a, b, z)]
    rows_near, ready = project(near, (0, 2, 3, 4), out_ids, qkv, weight=20)
    near_swap = [trade(after(t, ready), "core") for t in near]
    late = [after(t, ready) for t in (ab, bz, az, abz)]
    late_swap = [trade(t, "core") for t in late]
    places = (8, 10, 11, 12, 1, 7, 5, 6, 9, 15, 13, 14)
    (proj,) = project(near_swap + late + late_swap, places, out_ids, qkv, before=rows_near)
    return (out[None], proj[None])


def solution(mesh):
    fine = Mesh(mesh.devices.reshape((4, 4) + SIZES), ("dp", "pipe") + AXES)
    return jax.shard_map(
        shards,
        mesh=fine,
        in_specs=(
            P("pipe", "dp", AXES),
            P("pipe", ("dp",) + AXES, None),
            P("pipe", None),
            P("pipe", AXES, None),
            P("pipe", None, AXES),
        ),
        out_specs=(P("pipe", ("dp",) + AXES, None), P("pipe", "dp", AXES)),
        check_vma=False,
    )
```

```python
import functools
import itertools

import jax
import jax.numpy as jnp
from jax import lax
from jax.experimental import pallas as pl
from jax.experimental.pallas import tpu as pltpu
from jax.sharding import Mesh, PartitionSpec as P

AXES = ("x", "z", "core")
SIZES = (4, 2, 2)
TRADES = {
    "o": ((0, 0), 0, 0),
    "a": ((1, 3), 0, 0),
    "b": ((3, 1), 0, 0),
    "z": ((0, 0), 1, 0),
    "ab": ((2, 2), 0, 0),
    "az": ((1, 3), 1, 0),
    "bz": ((3, 1), 1, 0),
    "abz": ((2, 2), 1, 0),
    "core": ((0, 0), 0, 1),
}
FIRST = ("abz", "bz", "az", "a")
SECOND = ("ab", "b", "z", "o")
GATHERED = ("o", "ab", "a", "b", "z", "az", "abz", "bz")


def trade(value, name):
    x_mask, z_mask, core_mask = TRADES[name]
    pairs = []
    for x, z, c in itertools.product(*map(range, SIZES)):
        to = ((x ^ x_mask[c]) * 2 + (z ^ z_mask)) * 2 + (c ^ core_mask)
        pairs.append(((x * 2 + z) * 2 + c, to))
    return lax.ppermute(value, AXES, pairs)


def next_section(value):
    count = lax.axis_size("pipe")
    return lax.ppermute(value, "pipe", [(s, (s + 1) % count) for s in range(count)])


def after(value, *others):
    return lax.optimization_barrier((value,) + others)[0]


def normalize(values, gain_row):
    wide = values.astype(jnp.float32)
    scaler = lax.rsqrt(jnp.mean(wide * wide, axis=-1, keepdims=True) + 1e-05)
    return (wide * scaler * gain_row).astype(jnp.bfloat16)


def block_ids(names):
    x, z, core = (lax.axis_index(a) for a in AXES)
    ids = []
    for c in (core, 1 - core):
        for name in names:
            (m0, m1), zm, _ = TRADES[name]
            m = m0 + (m1 - m0) * c
            ids.append(((x ^ m) * 2 + (z ^ zm)) * 2 + c)
    return jnp.stack(ids).astype(jnp.int32)


def pick_kernel(ids, hid_ref, mine_ref, theirs_ref):
    rows = hid_ref.shape[0] // 16
    for i in range(16):
        start = pl.multiple_of(ids[i] * rows, rows)
        out = (mine_ref, theirs_ref)[i // 8]
        out[i % 8 * rows : (i % 8 + 1) * rows, :] = hid_ref[pl.ds(start, rows), :]


def pick(ids, hid):
    rows, depth = hid.shape
    return pl.pallas_call(
        pick_kernel,
        out_shape=[jax.ShapeDtypeStruct((rows // 2, depth), jnp.bfloat16)] * 2,
        in_specs=[pl.BlockSpec(memory_space=pltpu.SMEM), pl.BlockSpec(memory_space=pltpu.VMEM)],
        out_specs=[pl.BlockSpec(memory_space=pltpu.VMEM)] * 2,
        compiler_params=pltpu.CompilerParams(vmem_limit_bytes=4 << 20),
        cost_estimate=pl.CostEstimate(flops=0, bytes_accessed=4 * rows * depth, transcendentals=0),
    )(ids, hid)


def product(parts, w_ref):
    deep = w_ref.shape[0] // 4
    total = None
    for i in range(4):
        at = slice(i * deep, (i + 1) * deep)
        lhs = jnp.concatenate([p[:, at] for p in parts], axis=0)
        term = jnp.dot(lhs, w_ref[at, :], preferred_element_type=jnp.float32)
        total = term if total is None else total + term
    return total.astype(jnp.bfloat16)


def project_kernel(places, first, ids, w_ref, *refs):
    rows_ref, sem = refs[-2:]
    parts = refs[:-4] if first else refs[1:-3]
    out_ref = refs[-4] if first else refs[-3]
    rows = rows_ref.shape[0] // len(places)
    rows_ref[...] = product(parts, w_ref)
    copies = []
    for i, at in enumerate(places):
        start = pl.multiple_of(ids[at] * rows, rows)
        copies.append(
            pltpu.make_async_copy(
                rows_ref.at[pl.ds(i * rows, rows), :], out_ref.at[pl.ds(start, rows), :], sem.at[i]
            )
        )
    for c in copies:
        c.start()
    if first:
        refs[-3][...] = jnp.zeros_like(refs[-3])
    for c in copies:
        c.wait()


def project(pieces, places, ids, w, before=None, weight=1):
    rows = pieces[0].shape[0]
    depth, width = w.shape
    n = len(pieces)
    extra = [] if before is None else [before]
    vmem = pl.BlockSpec(memory_space=pltpu.VMEM)
    anywhere = pl.BlockSpec(memory_space=pl.ANY)
    return pl.pallas_call(
        functools.partial(project_kernel, places, before is None),
        out_shape=[
            jax.ShapeDtypeStruct((16 * rows, width), jnp.bfloat16),
            jax.ShapeDtypeStruct((8, 128), jnp.float32),
        ][: 2 - len(extra)],
        in_specs=[pl.BlockSpec(memory_space=pltpu.SMEM), vmem] + [anywhere] * len(extra) + [vmem] * n,
        out_specs=[anywhere, vmem][: 2 - len(extra)],
        scratch_shapes=[
            pltpu.VMEM((n * rows, width), jnp.bfloat16),
            pltpu.SemaphoreType.DMA((n,)),
        ],
        input_output_aliases={2: 0} if extra else {},
        compiler_params=pltpu.CompilerParams(vmem_limit_bytes=16 << 20),
        cost_estimate=pl.CostEstimate(
            flops=weight * 2 * n * rows * depth * width,
            bytes_accessed=2 * (n * rows * depth + depth * width + n * rows * width),
            transcendentals=0,
        ),
    )(ids, w, *extra, *pieces)


def dot_bf16(a, b):
    return jnp.dot(a, b, preferred_element_type=jnp.float32).astype(jnp.bfloat16)


def add(*terms):
    return sum(t.astype(jnp.float32) for t in terms)


def shards(hidden, residual, norm_gain, down_weight, qkv_weight):
    resid = residual[0]
    gain = norm_gain[0]
    qkv = qkv_weight[0]
    down = down_weight[0]
    rows = resid.shape[0]
    half = 4 * rows
    mine, theirs = pick(block_ids(FIRST + SECOND), hidden[0])
    out_ids = block_ids(GATHERED)

    sent = lax.optimization_barrier(dot_bf16(theirs, down))
    first, second = (lax.optimization_barrier(s) for s in (sent[:half], sent[half:]))
    kept = lax.optimization_barrier(dot_bf16(mine, down))
    got = trade(first, "core")

    def both(lo, hi):
        at = slice(lo * rows, hi * rows)
        return lax.optimization_barrier(add(kept[at], got[at]).astype(jnp.bfloat16))

    abz, az_a, bz = both(0, 1), both(2, 4), both(1, 2)
    for_ab = trade(abz, "z")
    for_z_o = trade(az_a, "a")
    for_b = trade(bz, "z")
    got = trade(second, "core")
    own = [(kept[half + i * rows : half + (i + 1) * rows], got[i * rows : (i + 1) * rows]) for i in range(4)]
    ab = lax.optimization_barrier(add(*own[0], for_ab).astype(jnp.bfloat16))
    last_ab = trade(ab, "ab")
    z = lax.optimization_barrier(add(*own[2], after(for_z_o, ab)[:rows]).astype(jnp.bfloat16))
    last_z = trade(z, "z")
    b = lax.optimization_barrier(add(*own[1], after(for_b, z)).astype(jnp.bfloat16))
    last_b = trade(b, "b")
    out = add(resid, *own[3], for_z_o[rows:], last_ab, last_z, last_b).astype(jnp.bfloat16)
    out = lax.optimization_barrier(out)

    normed = lax.optimization_barrier(normalize(next_section(out), gain))
    b = trade(normed, "b")
    z = trade(normed, "z")
    a = trade(normed, "a")
    abz = trade(z, "ab")
    az = trade(z, "a")
    ab = trade(b, "a")
    bz = trade(b, "z")
    near = [after(t, a, b, z) for t in (normed, a, b, z)]
    rows_near, ready = project(near, (0, 2, 3, 4), out_ids, qkv, weight=20)
    near_swap = [trade(after(t, ready), "core") for t in near]
    late = [after(t, ready) for t in (abz, bz, ab, az)]
    late_swap = [trade(t, "core") for t in late]
    places = (8, 10, 11, 12, 6, 7, 1, 5, 14, 15, 9, 13)
    (proj,) = project(near_swap + late + late_swap, places, out_ids, qkv, before=rows_near)
    return (out[None], proj[None])


def solution(mesh):
    fine = Mesh(mesh.devices.reshape((4, 4) + SIZES), ("dp", "pipe") + AXES)
    return jax.shard_map(
        shards,
        mesh=fine,
        in_specs=(
            P("pipe", "dp", AXES),
            P("pipe", ("dp",) + AXES, None),
            P("pipe", None),
            P("pipe", AXES, None),
            P("pipe", None, AXES),
        ),
        out_specs=(P("pipe", ("dp",) + AXES, None), P("pipe", "dp", AXES)),
        check_vma=False,
    )
```
